32 devices in a mesh: snap: 2 (over y), row: 4 (over z), col: 4 (over x, core).
Axes of the slice: x: 2, y: 2, z: 4, core: 2. Of those that a mesh axis runs over, the one named last changes fastest.
Arguments:
- orbitals: float32 [12288, 768], P(('snap', 'row', 'col')), parts along dimension 0, may hold values from -6 to 6
- screened: float32 [6, 6144, 6144], P('snap', 'row', 'col'), parts along dimension 0, may hold values from -0.0029296875 to 0.0029296875
- green_weight: float32 [6, 768], P('snap'), parts along dimension 0, may hold values from 0.05 to 1
- time_weight: float32 [3], replicated, may hold values from 0.3 to 1
Outputs:
- updated: float32 [12288, 768], P(('snap', 'row', 'col')), parts along dimension 0
The draws below stay inside these ranges and needn't reach their ends.
There are 2 independent parts, one for each index of `snap`. The reference program is written for one: setup_inputs(seed, part) draws one part's arguments, and reference() takes and returns one part's arrays. A program takes and returns all parts, laid end to end along the dimension named above; an argument that names none is the same for every part. Nothing has to cross between parts.
All inputs are finite; a program needn't handle non-finite values.
Results may differ from the reference program's by a relative error of at most 0.00013.
Values sent between devices are 32-bit elements; how exact they have to be, the bound alone decides.
A program may use at most 128 MiB of HBM per device.

```python
import math
import jax
import jax.numpy as jnp
from jax import lax

NP = 6144
NORB = 768
TIMES = 3
PASSES = 2


def level_of(stream_key, shape, split, smallest, high):
    gain = 1.0
    for axis_at, parts in split:
        steps = jax.random.uniform(jax.random.fold_in(jax.random.fold_in(stream_key, 6), axis_at), (parts,), jnp.float32, smallest / len(split), high / len(split))
        gain = gain * jnp.repeat(jnp.exp(steps), shape[axis_at] // parts).reshape((-1,) + (1,) * (len(shape) - 1 - axis_at))
    return gain


def centred(key, dims, scale, bound, cuts=(), dtype=jnp.bfloat16):
    array = jax.random.normal(key, dims, jnp.float32) * scale
    if len(cuts) > 0:
        array = level_of(key, dims, cuts, -0.22, 0.18) * array
    return jnp.clip(array, min=-bound, max=bound).astype(dtype)


def setup_inputs(seed: int = 0, part: int = 0) -> dict:
    streams_of = jax.random.split(jax.random.key(seed), 5)
    part_splits = jax.random.split(jax.random.fold_in(streams_of[4], part), 5)
    orbitals = centred(part_splits[0], (NP, NORB), 1.0, 6.0, ((0, 16),), jnp.float32)
    screened = centred(part_splits[1], (TIMES, NP, NP), (NP * NORB) ** -0.5, 0.0029296875, ((1, 4), (2, 4)), jnp.float32)
    green_weight = jnp.clip(jnp.exp(jax.random.uniform(part_splits[2], (TIMES, NORB), jnp.float32, math.log(0.05), math.log(1.0))), 0.05, 1.0)
    time_weight = jnp.clip(jax.random.uniform(streams_of[3], (TIMES,), jnp.float32, 0.3, 1.0), 0.3, 1.0)
    return dict(orbitals=orbitals, screened=screened, green_weight=green_weight, time_weight=time_weight)


def reference(orbitals, screened, green_weight, time_weight):
    phi = orbitals
    for step in range(PASSES):
        correction = jnp.zeros(phi.shape, jnp.float32)
        for t in range(TIMES):
            green = lax.dot_general(phi * green_weight[t], phi, (((1,), (1,)), ((), ())), precision=lax.Precision.HIGHEST, preferred_element_type=jnp.float32)
            applied = jnp.dot(green * screened[t], phi, precision=lax.Precision.HIGHEST, preferred_element_type=jnp.float32)
            correction = correction + time_weight[t] * applied
        phi = phi - correction
    return phi
```

```python
import functools

import jax
import jax.numpy as jnp
from jax import lax
from jax.experimental import pallas as pl
from jax.experimental.pallas import tpu as pltpu
from jax.sharding import PartitionSpec as P

PASSES = 2
LANES = 128


def split(value):
    high = value.astype(jnp.bfloat16)
    low = (value - high.astype(jnp.float32)).astype(jnp.bfloat16)
    return high, low


def apply_kernel(times, parts, has_total, index_ref, *refs):
    rows_refs, refs = refs[:parts], refs[parts:]
    cols_refs, refs = refs[:parts], refs[parts:]
    weight_ref, screened_ref, refs = refs[0], refs[1], refs[2:]
    total_refs = None
    if has_total:
        total_refs, refs = refs[:parts], refs[parts:]
    out_refs, (weighted, plain) = refs[:parts], refs[parts:]

    @pl.when(pl.program_id(0) == 0)
    def _():
        cols = jnp.concatenate([ref[...] for ref in cols_refs], axis=1)
        width, depth = cols.shape
        high, low = split(cols)
        plain[0:width, :] = high
        plain[width : 2 * width, :] = high
        plain[2 * width : 3 * width, :] = low
        for t in range(times):
            high, low = split((cols * weight_ref[t : t + 1, :]).T)
            weighted[t, 0:depth, :] = high
            weighted[t, depth : 2 * depth, :] = high
            weighted[t, 2 * depth : 3 * depth, :] = low

    high, low = split(jnp.concatenate([ref[...] for ref in rows_refs], axis=1))
    rows = jnp.concatenate([high, low, high], axis=1)
    mixed = None
    for t in range(times):
        green = jnp.dot(rows, weighted[t], preferred_element_type=jnp.float32)
        term = green * screened_ref[t]
        mixed = term if mixed is None else mixed + term
    high, low = split(mixed)
    mixed = jnp.concatenate([high, low, high], axis=1)
    applied = jnp.dot(mixed, plain[...], preferred_element_type=jnp.float32)
    part = applied.shape[1] // parts
    for k in range(parts):
        value = applied[:, k * part : (k + 1) * part]
        out_refs[k][...] = value + total_refs[k][...] if has_total else value


def apply_block(index, rows, cols, weight, screened, total):
    times = screened.shape[0]
    parts = len(rows)
    n_rows, part = rows[0].shape
    depth = parts * part
    width = cols[0].shape[0]
    tile = next(k for k in (512, 384, 256, 128, n_rows) if n_rows % k == 0)
    row_spec = pl.BlockSpec((tile, part), lambda i, ix: (i, 0))
    in_specs = [row_spec] * parts
    in_specs += [pl.BlockSpec((width, part), lambda i, ix: (0, 0))] * parts
    in_specs += [
        pl.BlockSpec((times, depth), lambda i, ix: (0, 0)),
        pl.BlockSpec((times, tile, width), lambda i, ix: (0, i, ix[0])),
    ]
    args = [index, *rows, *cols, weight, screened]
    if total is not None:
        in_specs += [row_spec] * parts
        args += total
    return pl.pallas_call(
        functools.partial(apply_kernel, times, parts, total is not None),
        out_shape=[jax.ShapeDtypeStruct((n_rows, part), jnp.float32)] * parts,
        grid_spec=pltpu.PrefetchScalarGridSpec(
            num_scalar_prefetch=1,
            grid=(n_rows // tile,),
            in_specs=in_specs,
            out_specs=[row_spec] * parts,
            scratch_shapes=[
                pltpu.VMEM((times, 3 * depth, width), jnp.bfloat16),
                pltpu.VMEM((3 * width, depth), jnp.bfloat16),
            ],
        ),
        compiler_params=pltpu.CompilerParams(
            dimension_semantics=("arbitrary",), vmem_limit_bytes=56 * 1024 * 1024
        ),
        cost_estimate=pl.CostEstimate(
            flops=6 * (times + 1) * n_rows * width * depth,
            bytes_accessed=4 * (times * n_rows * width + 3 * n_rows * depth),
            transcendentals=0,
        ),
    )(*args)


def chain_kernel(
    times, own_ref, weight_ref, screened_ref, out_ref,
    buf, side, rows, weighted, plain, acc, from_partner, from_twin, tiles,
    own_sem, row_recv, col_recv, side_recv, partner_recv, twin_recv, tile_sem,
    partner_send, twin_send, relay_send, down_send, up_send,
    side_send, cross_send, sum_send, twin_sum_send,
):
    n = lax.axis_size("row")
    r = lax.axis_index("row")
    c = lax.axis_index("col")
    x, k = c // 2, c % 2
    partner, twin, opposite = c + 1 - 2 * k, c + 2 - 4 * x, 3 - c
    slots, chunk, depth = buf.shape
    slots = slots // 2
    pieces = slots // n
    points = pieces * chunk
    units = slots // 2
    diagonal = r == c
    base = jnp.where(diagonal, 0, slots)
    end_set = (c == 0) | (c == n - 1)
    goes_down = (r >= c) & (r < n - 1)
    goes_up = (r <= c) & (r > 0)
    relays = (goes_down | goes_up) & jnp.logical_not(diagonal)
    distance = jnp.where(r > c, r - c, c - r)
    near = relays & (distance == 1)
    side_set = (n - 1) * (1 - x)
    side_next = r + 2 * x - 1
    side_goes = (side_next >= 0) & (side_next < n)
    side_source = r == side_set

    def remote(source, target, send, recv, row, col):
        return pltpu.make_async_remote_copy(
            src_ref=source, dst_ref=target, send_sem=send, recv_sem=recv,
            device_id={"row": row, "col": col}, device_id_type=pl.DeviceIdType.MESH,
        )

    def to_partner(i):
        q = c * pieces + i
        return remote(buf.at[q], buf.at[q], partner_send.at[i], row_recv.at[q], r, partner)

    def to_twin(i):
        q = c * pieces + i
        return remote(buf.at[q], buf.at[q], twin_send.at[i], row_recv.at[q], r, twin)

    def relay(i):
        q = twin * pieces + i
        return remote(buf.at[q], buf.at[q], relay_send.at[i], row_recv.at[q], r, partner)

    def wait_row(col, i):
        q = col * pieces + i
        remote(buf.at[q], buf.at[q], partner_send.at[i], row_recv.at[q], r, partner).wait_recv()

    def down(q):
        return remote(buf.at[base + q], buf.at[slots + q], down_send.at[q], col_recv.at[q], r + 1, c)

    def up(q):
        return remote(buf.at[base + q], buf.at[slots + q], up_send.at[q], col_recv.at[q], r - 1, c)

    def wait_col(q):
        remote(buf.at[slots + q], buf.at[slots + q], down_send.at[q], col_recv.at[q], r, partner).wait_recv()

    def forward(q, carried):
        @pl.when(goes_down & carried)
        def _():
            down(q).start()

        @pl.when(goes_up & carried)
        def _():
            up(q).start()

    def side_forward(i, source):
        return remote(source, side.at[i], side_send.at[i], side_recv.at[i], side_next, c)

    def side_cross(i):
        q = c * pieces + i
        return remote(side.at[i], buf.at[slots + q], cross_send.at[i], col_recv.at[q], r, side_set)

    def unit_slots(u):
        half = u // pieces
        block = 2 * ((x + half) % 2)
        return block * pieces + u % pieces, (block + 1) * pieces + u % pieces

    def serve(u):
        carried = jnp.logical_not(end_set) | (u < pieces)
        for q in unit_slots(u):
            wait_col(q)
            forward(q, carried)

    def tile_of(m):
        return 2 * ((x + 1 + m // 2) % 2) + (k + 1 + m) % 2

    def tile_copies(step):
        u, m = step // n, step % n
        slot = step % 2
        first = pl.multiple_of(tile_of(m) * points, chunk)
        return [
            pltpu.make_async_copy(
                screened_ref.at[:, pl.ds(first, points), pl.ds(pl.multiple_of(q * chunk, chunk), chunk)],
                tiles.at[slot, :, :, pl.ds(j * chunk, chunk)],
                tile_sem.at[slot, j],
            )
            for j, q in enumerate(unit_slots(u))
        ]

    def split_rows(col):
        @pl.loop(0, pieces)
        def _(i):
            q = col * pieces + i
            first = pl.multiple_of(q * chunk, chunk)
            high, low = split(buf[q])
            rows[pl.ds(first, chunk), 0:depth] = high
            rows[pl.ds(first, chunk), depth : 2 * depth] = low
            rows[pl.ds(first, chunk), 2 * depth : 3 * depth] = high

    def partner_sum(j):
        block = opposite if j == 0 else partner
        return remote(acc.at[block], from_partner.at[j], sum_send.at[j], partner_recv.at[j], r, partner)

    def twin_sum(i):
        part = pl.ds(i * chunk, chunk)
        return remote(acc.at[twin, part], from_twin.at[part], twin_sum_send.at[i], twin_recv.at[i], r, twin)

    own_copy = pltpu.make_async_copy(own_ref, buf.at[pl.ds(c * pieces, pieces)], own_sem)
    own_copy.start()
    for copy in tile_copies(0):
        copy.start()

    barrier = pltpu.get_barrier_semaphore()
    for col in (partner, twin, opposite):
        pl.semaphore_signal(
            barrier, inc=1, device_id={"row": r, "col": col}, device_id_type=pl.DeviceIdType.MESH
        )

    @pl.when(r > 0)
    def _():
        pl.semaphore_signal(
            barrier, inc=1, device_id={"row": r - 1, "col": c}, device_id_type=pl.DeviceIdType.MESH
        )

    @pl.when(r < n - 1)
    def _():
        pl.semaphore_signal(
            barrier, inc=1, device_id={"row": r + 1, "col": c}, device_id_type=pl.DeviceIdType.MESH
        )

    own_copy.wait()
    pl.semaphore_wait(barrier, 3 + jnp.where(r > 0, 1, 0) + jnp.where(r < n - 1, 1, 0))

    for i in range(pieces):
        to_twin(i).start()
        to_partner(i).start()

        @pl.when(side_source & side_goes)
        def _():
            side_forward(i, buf.at[c * pieces + i]).start()

        @pl.when(diagonal)
        def _():
            forward(c * pieces + i, True)

    acc[...] = jnp.zeros_like(acc)
    split_rows(c)
    for i in range(pieces):
        wait_row(partner, i)

        @pl.when(diagonal)
        def _():
            forward(partner * pieces + i, True)

    split_rows(partner)
    middle = jnp.logical_not(end_set)
    for i in range(pieces):
        wait_row(twin, i)
        relay(i).start()

        @pl.when(diagonal)
        def _():
            forward(twin * pieces + i, middle)

        wait_row(opposite, i)

        @pl.when(diagonal)
        def _():
            forward(opposite * pieces + i, middle)

        @pl.when(jnp.logical_not(side_source))
        def _():
            pltpu.make_async_remote_copy(
                src_ref=side.at[i], dst_ref=side.at[i], send_sem=side_send.at[i],
                recv_sem=side_recv.at[i], device_id={"row": r, "col": partner},
                device_id_type=pl.DeviceIdType.MESH,
            ).wait_recv()

            @pl.when(side_goes)
            def _():
                side_forward(i, side.at[i]).start()

            side_cross(i).start()

        if i > 0:
            @pl.when(near)
            def _():
                serve(i - 1)

    split_rows(twin)
    split_rows(opposite)

    @pl.when(relays & jnp.logical_not(near))
    def _():
        serve(0)

    ahead = jnp.where(near, 2, 1)
    steps = units * n

    @pl.loop(0, units)
    def _(u):
        @pl.when(jnp.logical_not(diagonal) & jnp.logical_not(relays))
        def _():
            for q in unit_slots(u):
                wait_col(q)

        first, second = unit_slots(u)
        cols = jnp.concatenate([buf[base + first], buf[base + second]], axis=0)
        width = cols.shape[0]
        high, low = split(cols)
        plain[0:width, :] = high
        plain[width : 2 * width, :] = high
        plain[2 * width : 3 * width, :] = low
        turned = cols.T
        for t in range(times):
            high, low = split(turned * weight_ref[:, t : t + 1])
            weighted[t, 0:depth, :] = high
            weighted[t, depth : 2 * depth, :] = high
            weighted[t, 2 * depth : 3 * depth, :] = low

        @pl.loop(0, n)
        def _(m):
            step = u * n + m

            @pl.when((m == n // 2) & relays & (u + ahead < units))
            def _():
                serve(u + ahead)

            @pl.when(step + 1 < steps)
            def _():
                for copy in tile_copies(step + 1):
                    copy.start()

            for copy in tile_copies(step):
                copy.wait()
            tile = tile_of(m)
            left = rows[pl.ds(pl.multiple_of(tile * points, chunk), points), :]
            mixed = None
            for t in range(times):
                green = jnp.dot(left, weighted[t], preferred_element_type=jnp.float32)
                term = green * tiles[step % 2, t]
                mixed = term if mixed is None else mixed + term
            high, low = split(mixed)
            mixed = jnp.concatenate([high, low, high], axis=1)
            acc[tile] = acc[tile] + jnp.dot(mixed, plain[...], preferred_element_type=jnp.float32)

            @pl.when((u == units - 1) & (m == 0))
            def _():
                partner_sum(0).start()

            @pl.when((u == units - 1) & (m == 1))
            def _():
                partner_sum(0).wait_recv()
                for i in range(pieces):
                    part = slice(i * chunk, (i + 1) * chunk)
                    acc[twin, part, :] = acc[twin, part, :] + from_partner[0, part, :]
                    twin_sum(i).start()

            @pl.when((u == units - 1) & (m == 2))
            def _():
                partner_sum(1).start()

    partner_sum(1).wait_recv()
    for i in range(pieces):
        part = slice(i * chunk, (i + 1) * chunk)
        mine = acc[c, part, :] + from_partner[1, part, :]
        twin_sum(i).wait_recv()
        out_ref[part, :] = buf[c * pieces + i] - (mine + from_twin[part, :])

    for i in range(pieces):
        to_twin(i).wait_send()
        to_partner(i).wait_send()
        relay(i).wait_send()
        twin_sum(i).wait_send()

        @pl.when(side_goes)
        def _():
            side_forward(i, side.at[i]).wait_send()

        @pl.when(jnp.logical_not(side_source))
        def _():
            side_cross(i).wait_send()

    for j in range(2):
        partner_sum(j).wait_send()
    for q in range(slots):
        carried = middle | (x == q // (2 * pieces))

        @pl.when(goes_down & carried)
        def _():
            down(q).wait_send()

        @pl.when(goes_up & carried)
        def _():
            up(q).wait_send()


def chain_pass(step, orbitals, weight, screened):
    times, n_rows, n_cols = screened.shape
    points, depth = orbitals.shape
    n = n_rows // points
    pieces = 3
    chunk = points // pieces
    slots = n * pieces
    dma = pltpu.SemaphoreType.DMA
    return pl.pallas_call(
        functools.partial(chain_kernel, times),
        out_shape=jax.ShapeDtypeStruct((points, depth), jnp.float32),
        in_specs=[
            pl.BlockSpec(memory_space=pl.ANY),
            pl.BlockSpec(memory_space=pltpu.VMEM),
            pl.BlockSpec(memory_space=pl.ANY),
        ],
        out_specs=pl.BlockSpec(memory_space=pltpu.VMEM),
        scratch_shapes=[
            pltpu.VMEM((2 * slots, chunk, depth), jnp.float32),
            pltpu.VMEM((pieces, chunk, depth), jnp.float32),
            pltpu.VMEM((n_rows, 3 * depth), jnp.bfloat16),
            pltpu.VMEM((times, 3 * depth, 2 * chunk), jnp.bfloat16),
            pltpu.VMEM((6 * chunk, depth), jnp.bfloat16),
            pltpu.VMEM((n, points, depth), jnp.float32),
            pltpu.VMEM((2, points, depth), jnp.float32),
            pltpu.VMEM((points, depth), jnp.float32),
            pltpu.VMEM((2, times, points, 2 * chunk), jnp.float32),
            dma(()), dma((slots,)), dma((slots,)), dma((pieces,)), dma((2,)), dma((pieces,)), dma((2, 2)),
            dma((pieces,)), dma((pieces,)), dma((pieces,)), dma((slots,)), dma((slots,)),
            dma((pieces,)), dma((pieces,)), dma((2,)), dma((pieces,)),
        ],
        compiler_params=pltpu.CompilerParams(
            collective_id=step, has_side_effects=True, vmem_limit_bytes=60 * 1024 * 1024
        ),
        cost_estimate=pl.CostEstimate(
            flops=6 * (times + 1) * n_rows * n_cols * depth,
            bytes_accessed=4 * times * n_rows * n_cols,
            transcendentals=0,
        ),
    )(orbitals.reshape(pieces, chunk, depth), weight.T, screened)


def scatter_rows(value):
    n_col = lax.axis_size("col")
    if n_col & (n_col - 1):
        return lax.psum_scatter(value, "col", scatter_dimension=0, tiled=True)
    me = lax.axis_index("col")
    points = value.shape[0] // n_col
    value = value.reshape(n_col, points, value.shape[1])
    distance = 1
    while distance < n_col:
        bit = (me // distance) % 2
        pairs = value.reshape((value.shape[0] // 2, 2) + value.shape[1:])
        mine = lax.dynamic_index_in_dim(pairs, bit, 1, keepdims=False)
        theirs = lax.dynamic_index_in_dim(pairs, 1 - bit, 1, keepdims=False)
        swap = [(k, k ^ distance) for k in range(n_col)]
        value = mine + lax.ppermute(theirs, "col", swap)
        distance *= 2
    return value[0]


def body(orbitals, screened, green_weight, time_weight):
    n_row = lax.axis_size("row")
    n_col = lax.axis_size("col")
    factor = n_col // n_row
    points, depth = orbitals.shape
    weight = green_weight * time_weight[:, None]
    if n_row == 4 and n_col == 4 and points % 3 == 0 and (points // 3) % LANES == 0:
        for step in range(PASSES):
            orbitals = chain_pass(step, orbitals, weight, screened)
        return orbitals
    to_columns = [
        ((c // factor) * n_col + (c % factor) * n_row + m, m * n_col + c)
        for m in range(n_row)
        for c in range(n_col)
    ]
    ring = [(k, (k + 1) % n_row) for k in range(n_row)]
    me = lax.axis_index("row")
    parts = 1
    own = jnp.split(orbitals, parts, axis=1)
    for step in range(PASSES):
        piece = [lax.ppermute(o, ("row", "col"), to_columns) for o in own]
        rows = [lax.all_gather(o, "col", axis=0, tiled=True) for o in own]
        total = None
        if points % 128 == 0:
            for hop in range(n_row):
                later = None
                if hop < n_row - 1:
                    if total is not None:
                        piece, total = lax.optimization_barrier((piece, total))
                    later = [lax.ppermute(p, "row", ring) for p in piece]
                index = lax.rem(me - hop + n_row, n_row).astype(jnp.int32).reshape(1)
                total = apply_block(index, rows, piece, weight, screened, total)
                piece = later
        else:
            columns = [lax.all_gather(p, "row", axis=0, tiled=True) for p in piece]
            index = jnp.zeros((1,), jnp.int32)
            total = apply_block(index, rows, columns, weight, screened, None)
        own = [
            o - scatter_rows(v)
            for o, v in zip(own, total)
        ]
    return jnp.concatenate(own, axis=1)


def solution(mesh):
    in_specs = (P(("snap", "row", "col"), None), P("snap", "row", "col"), P("snap", None), P())
    out_specs = P(("snap", "row", "col"), None)
    return jax.shard_map(body, mesh=mesh, in_specs=in_specs, out_specs=out_specs, check_vma=False)
```

```python
import functools

import jax
import jax.numpy as jnp
from jax import lax
from jax.experimental import pallas as pl
from jax.experimental.pallas import tpu as pltpu
from jax.sharding import PartitionSpec as P

PASSES = 2
LANES = 128


def split(value):
    high = value.astype(jnp.bfloat16)
    low = (value - high.astype(jnp.float32)).astype(jnp.bfloat16)
    return high, low


def apply_kernel(times, parts, has_total, index_ref, *refs):
    rows_refs, refs = refs[:parts], refs[parts:]
    cols_refs, refs = refs[:parts], refs[parts:]
    weight_ref, screened_ref, refs = refs[0], refs[1], refs[2:]
    total_refs = None
    if has_total:
        total_refs, refs = refs[:parts], refs[parts:]
    out_refs, (weighted, plain) = refs[:parts], refs[parts:]

    @pl.when(pl.program_id(0) == 0)
    def _():
        cols = jnp.concatenate([ref[...] for ref in cols_refs], axis=1)
        width, depth = cols.shape
        high, low = split(cols)
        plain[0:width, :] = high
        plain[width : 2 * width, :] = high
        plain[2 * width : 3 * width, :] = low
        for t in range(times):
            high, low = split((cols * weight_ref[t : t + 1, :]).T)
            weighted[t, 0:depth, :] = high
            weighted[t, depth : 2 * depth, :] = high
            weighted[t, 2 * depth : 3 * depth, :] = low

    high, low = split(jnp.concatenate([ref[...] for ref in rows_refs], axis=1))
    rows = jnp.concatenate([high, low, high], axis=1)
    mixed = None
    for t in range(times):
        green = jnp.dot(rows, weighted[t], preferred_element_type=jnp.float32)
        term = green * screened_ref[t]
        mixed = term if mixed is None else mixed + term
    high, low = split(mixed)
    mixed = jnp.concatenate([high, low, high], axis=1)
    applied = jnp.dot(mixed, plain[...], preferred_element_type=jnp.float32)
    part = applied.shape[1] // parts
    for k in range(parts):
        value = applied[:, k * part : (k + 1) * part]
        out_refs[k][...] = value + total_refs[k][...] if has_total else value


def apply_block(index, rows, cols, weight, screened, total):
    times = screened.shape[0]
    parts = len(rows)
    n_rows, part = rows[0].shape
    depth = parts * part
    width = cols[0].shape[0]
    tile = next(k for k in (512, 384, 256, 128, n_rows) if n_rows % k == 0)
    row_spec = pl.BlockSpec((tile, part), lambda i, ix: (i, 0))
    in_specs = [row_spec] * parts
    in_specs += [pl.BlockSpec((width, part), lambda i, ix: (0, 0))] * parts
    in_specs += [
        pl.BlockSpec((times, depth), lambda i, ix: (0, 0)),
        pl.BlockSpec((times, tile, width), lambda i, ix: (0, i, ix[0])),
    ]
    args = [index, *rows, *cols, weight, screened]
    if total is not None:
        in_specs += [row_spec] * parts
        args += total
    return pl.pallas_call(
        functools.partial(apply_kernel, times, parts, total is not None),
        out_shape=[jax.ShapeDtypeStruct((n_rows, part), jnp.float32)] * parts,
        grid_spec=pltpu.PrefetchScalarGridSpec(
            num_scalar_prefetch=1,
            grid=(n_rows // tile,),
            in_specs=in_specs,
            out_specs=[row_spec] * parts,
            scratch_shapes=[
                pltpu.VMEM((times, 3 * depth, width), jnp.bfloat16),
                pltpu.VMEM((3 * width, depth), jnp.bfloat16),
            ],
        ),
        compiler_params=pltpu.CompilerParams(
            dimension_semantics=("arbitrary",), vmem_limit_bytes=56 * 1024 * 1024
        ),
        cost_estimate=pl.CostEstimate(
            flops=6 * (times + 1) * n_rows * width * depth,
            bytes_accessed=4 * (times * n_rows * width + 3 * n_rows * depth),
            transcendentals=0,
        ),
    )(*args)


def chain_kernel(
    times, own_ref, weight_ref, screened_ref, out_ref,
    buf, rows, weighted, plain, acc, from_partner, from_twin, tiles,
    own_sem, row_recv, col_recv, side_recv, partner_recv, twin_recv, tile_sem,
    partner_send, twin_send, relay_send, down_send, up_send,
    side_down_send, side_up_send, cross_send, sum_send, twin_sum_send,
):
    n = lax.axis_size("row")
    r = lax.axis_index("row")
    c = lax.axis_index("col")
    x, k = c // 2, c % 2
    partner, twin, opposite = c + 1 - 2 * k, c + 2 - 4 * x, 3 - c
    pieces, chunk, depth = own_ref.shape
    slots = n * pieces
    points = pieces * chunk
    units = slots // 2
    half_units = units // 2
    diagonal = r == c
    base = jnp.where(diagonal, 0, slots)
    goes_down = (r >= c) & (r < n - 1)
    goes_up = (r <= c) & (r > 0)
    relays = (goes_down | goes_up) & jnp.logical_not(diagonal)
    distance = jnp.where(r > c, r - c, c - r)
    near = relays & (distance == 1)
    far = relays & jnp.logical_not(near)

    def remote(source, target, send, recv, row, col):
        return pltpu.make_async_remote_copy(
            src_ref=source, dst_ref=target, send_sem=send, recv_sem=recv,
            device_id={"row": row, "col": col}, device_id_type=pl.DeviceIdType.MESH,
        )

    def to_partner(i):
        q = c * pieces + i
        return remote(buf.at[q], buf.at[q], partner_send.at[i], row_recv.at[q], r, partner)

    def to_twin(i):
        q = c * pieces + i
        return remote(buf.at[q], buf.at[q], twin_send.at[i], row_recv.at[q], r, twin)

    def relay(i):
        q = twin * pieces + i
        return remote(buf.at[q], buf.at[q], relay_send.at[i], row_recv.at[q], r, partner)

    def wait_row(col, i):
        q = col * pieces + i
        remote(buf.at[q], buf.at[q], partner_send.at[i], row_recv.at[q], r, partner).wait_recv()

    def down(q):
        return remote(buf.at[base + q], buf.at[slots + q], down_send.at[q], col_recv.at[q], r + 1, c)

    def up(q):
        return remote(buf.at[base + q], buf.at[slots + q], up_send.at[q], col_recv.at[q], r - 1, c)

    def wait_col(q):
        remote(buf.at[slots + q], buf.at[slots + q], down_send.at[q], col_recv.at[q], r, partner).wait_recv()

    def forward(q):
        @pl.when(goes_down)
        def _():
            down(q).start()

        @pl.when(goes_up)
        def _():
            up(q).start()

    side_count = pieces - 1

    def side_set(e):
        return 2 * (1 - x) + e

    def side_goes_down(e):
        return (r >= side_set(e)) & (r < n - 1)

    def side_goes_up(e):
        return (r <= side_set(e)) & (r > 0)

    def side_source(e, i):
        own = c * pieces + i
        place = 2 * slots + e * side_count + i - 1
        return buf.at[jnp.where(r == side_set(e), own, place)]

    def side_down(e, i):
        j = e * side_count + i - 1
        return remote(side_source(e, i), buf.at[2 * slots + j], side_down_send.at[j], side_recv.at[j], r + 1, c)

    def side_up(e, i):
        j = e * side_count + i - 1
        return remote(side_source(e, i), buf.at[2 * slots + j], side_up_send.at[j], side_recv.at[j], r - 1, c)

    def side_cross(e, i):
        j = e * side_count + i - 1
        q = c * pieces + i
        return remote(buf.at[2 * slots + j], buf.at[slots + q], cross_send.at[j], col_recv.at[q], r, side_set(e))

    def side_forward(e, i):
        @pl.when(side_goes_down(e))
        def _():
            side_down(e, i).start()

        @pl.when(side_goes_up(e))
        def _():
            side_up(e, i).start()

    def side_serve(i):
        for e in range(2):
            @pl.when(r != side_set(e))
            def _():
                j = e * side_count + i - 1
                here = buf.at[2 * slots + j]
                remote(here, here, cross_send.at[j], side_recv.at[j], r, partner).wait_recv()
                side_forward(e, i)
                side_cross(e, i).start()

    def unit_slots(u):
        half = jnp.where((u == 2) | (u >= 4), 1, 0)
        piece = ((u + 1) // 2) % pieces
        block = 2 * ((x + half) % 2)
        return block * pieces + piece, (block + 1) * pieces + piece

    def serve(u):
        for q in unit_slots(u):
            wait_col(q)
            forward(q)

    def place_of(step):
        whole = half_units * n
        late = step - whole
        second = jnp.where(late < units, late, late - units)
        u = jnp.where(step < whole, step // n, half_units + second // 2)
        m = jnp.where(step < whole, step % n, second % 2 + jnp.where(late < units, 0, 2))
        return u, m

    def tile_of(m):
        return 2 * ((x + 1 + m // 2) % 2) + (k + 1 + m) % 2

    def tile_copies(step):
        u, m = place_of(step)
        slot = step % 2
        first = pl.multiple_of(tile_of(m) * points, chunk)
        return [
            pltpu.make_async_copy(
                screened_ref.at[:, pl.ds(first, points), pl.ds(pl.multiple_of(q * chunk, chunk), chunk)],
                tiles.at[slot, :, :, pl.ds(j * chunk, chunk)],
                tile_sem.at[slot, j],
            )
            for j, q in enumerate(unit_slots(u))
        ]

    def split_rows(col):
        @pl.loop(0, pieces)
        def _(i):
            q = col * pieces + i
            first = pl.multiple_of(q * chunk, chunk)
            high, low = split(buf[q])
            rows[pl.ds(first, chunk), 0:depth] = high
            rows[pl.ds(first, chunk), depth : 2 * depth] = low
            rows[pl.ds(first, chunk), 2 * depth : 3 * depth] = high

    def partner_sum(j):
        block = opposite if j == 0 else partner
        return remote(acc.at[block], from_partner.at[j], sum_send.at[j], partner_recv.at[j], r, partner)

    def twin_sum(i):
        part = pl.ds(i * chunk, chunk)
        return remote(acc.at[twin, part], from_twin.at[part], twin_sum_send.at[i], twin_recv.at[i], r, twin)

    own_copy = pltpu.make_async_copy(own_ref, buf.at[pl.ds(c * pieces, pieces)], own_sem)
    own_copy.start()
    for copy in tile_copies(0):
        copy.start()

    barrier = pltpu.get_barrier_semaphore()
    for col in (partner, twin, opposite):
        pl.semaphore_signal(
            barrier, inc=1, device_id={"row": r, "col": col}, device_id_type=pl.DeviceIdType.MESH
        )

    @pl.when(r > 0)
    def _():
        pl.semaphore_signal(
            barrier, inc=1, device_id={"row": r - 1, "col": c}, device_id_type=pl.DeviceIdType.MESH
        )

    @pl.when(r < n - 1)
    def _():
        pl.semaphore_signal(
            barrier, inc=1, device_id={"row": r + 1, "col": c}, device_id_type=pl.DeviceIdType.MESH
        )

    own_copy.wait()
    pl.semaphore_wait(barrier, 3 + jnp.where(r > 0, 1, 0) + jnp.where(r < n - 1, 1, 0))

    for i in range(pieces):
        to_twin(i).start()
        to_partner(i).start()

        @pl.when(diagonal)
        def _():
            forward(c * pieces + i)

    for i in range(1, pieces):
        for e in range(2):
            @pl.when(r == side_set(e))
            def _():
                side_forward(e, i)

    acc[...] = jnp.zeros_like(acc)
    for i in range(pieces):
        wait_row(partner, i)

        @pl.when(diagonal)
        def _():
            forward(partner * pieces + i)

    split_rows(c)
    split_rows(partner)
    for i in range(pieces):
        for col in (twin, opposite):
            wait_row(col, i)
            if col is twin:
                relay(i).start()
            if i == 0:
                @pl.when(diagonal)
                def _():
                    forward(col * pieces + i)

        if i > 0:
            @pl.when(near)
            def _():
                serve(i - 1)

    side_serve(1)
    split_rows(twin)
    split_rows(opposite)

    @pl.when(far)
    def _():
        serve(0)

    steps = units * n
    whole = half_units * n

    @pl.loop(0, steps)
    def _(step):
        u, m = place_of(step)
        keep = jnp.where(u < half_units, 0, u - half_units)

        for unit, near_step, far_step in ((1, steps, 4), (3, 5, 9), (5, 10, 15)):
            @pl.when(relays & (step == jnp.where(near, near_step, far_step)))
            def _():
                serve(unit)

        @pl.when(step == n)
        def _():
            side_serve(2)

        @pl.when(step + 1 < steps)
        def _():
            for copy in tile_copies(step + 1):
                copy.start()

        @pl.when((m == 0) & (step < whole + units))
        def _():
            first, second = unit_slots(u)

            @pl.when(jnp.logical_not(diagonal) & (jnp.logical_not(relays) | (u == 2) | (u == 4)))
            def _():
                wait_col(first)
                wait_col(second)

            cols = jnp.concatenate([buf[base + first], buf[base + second]], axis=0)
            width = cols.shape[0]
            high, low = split(cols)
            plain[keep, 0:width, :] = high
            plain[keep, width : 2 * width, :] = high
            plain[keep, 2 * width : 3 * width, :] = low
            turned = cols.T
            for t in range(times):
                high, low = split(turned * weight_ref[:, t : t + 1])
                weighted[keep, t, 0:depth, :] = high
                weighted[keep, t, depth : 2 * depth, :] = high
                weighted[keep, t, 2 * depth : 3 * depth, :] = low

        for copy in tile_copies(step):
            copy.wait()
        tile = tile_of(m)
        left = rows[pl.ds(pl.multiple_of(tile * points, chunk), points), :]
        mixed = None
        for t in range(times):
            green = jnp.dot(left, weighted[keep, t], preferred_element_type=jnp.float32)
            term = green * tiles[step % 2, t]
            mixed = term if mixed is None else mixed + term
        high, low = split(mixed)
        mixed = jnp.concatenate([high, low, high], axis=1)
        acc[tile] = acc[tile] + jnp.dot(mixed, plain[keep], preferred_element_type=jnp.float32)

        @pl.when((u == units - 1) & (m == 0))
        def _():
            partner_sum(0).start()

        @pl.when((u == units - 1) & (m == 1))
        def _():
            partner_sum(0).wait_recv()
            for i in range(pieces):
                part = slice(i * chunk, (i + 1) * chunk)
                acc[twin, part, :] = acc[twin, part, :] + from_partner[0, part, :]
                twin_sum(i).start()

        @pl.when((u == units - 1) & (m == 2))
        def _():
            partner_sum(1).start()

    partner_sum(1).wait_recv()
    for i in range(pieces):
        part = slice(i * chunk, (i + 1) * chunk)
        mine = acc[c, part, :] + from_partner[1, part, :]
        twin_sum(i).wait_recv()
        out_ref[part, :] = buf[c * pieces + i] - (mine + from_twin[part, :])

    for i in range(pieces):
        to_twin(i).wait_send()
        to_partner(i).wait_send()
        relay(i).wait_send()
        twin_sum(i).wait_send()

    for i in range(1, pieces):
        for e in range(2):
            @pl.when(side_goes_down(e))
            def _():
                side_down(e, i).wait_send()

            @pl.when(side_goes_up(e))
            def _():
                side_up(e, i).wait_send()

            @pl.when(r != side_set(e))
            def _():
                side_cross(e, i).wait_send()

    for j in range(2):
        partner_sum(j).wait_send()
    for u in (0, 1, 3, 5):
        for q in unit_slots(u):
            @pl.when(goes_down)
            def _():
                down(q).wait_send()

            @pl.when(goes_up)
            def _():
                up(q).wait_send()


def chain_pass(step, orbitals, weight, screened):
    times, n_rows, n_cols = screened.shape
    points, depth = orbitals.shape
    n = n_rows // points
    pieces = 3
    chunk = points // pieces
    slots = n * pieces
    dma = pltpu.SemaphoreType.DMA
    return pl.pallas_call(
        functools.partial(chain_kernel, times),
        out_shape=jax.ShapeDtypeStruct((points, depth), jnp.float32),
        in_specs=[
            pl.BlockSpec(memory_space=pl.ANY),
            pl.BlockSpec(memory_space=pltpu.VMEM),
            pl.BlockSpec(memory_space=pl.ANY),
        ],
        out_specs=pl.BlockSpec(memory_space=pltpu.VMEM),
        scratch_shapes=[
            pltpu.VMEM((2 * slots + 2 * (pieces - 1), chunk, depth), jnp.float32),
            pltpu.VMEM((n_rows, 3 * depth), jnp.bfloat16),
            pltpu.VMEM((pieces, times, 3 * depth, 2 * chunk), jnp.bfloat16),
            pltpu.VMEM((pieces, 6 * chunk, depth), jnp.bfloat16),
            pltpu.VMEM((n, points, depth), jnp.float32),
            pltpu.VMEM((2, points, depth), jnp.float32),
            pltpu.VMEM((points, depth), jnp.float32),
            pltpu.VMEM((2, times, points, 2 * chunk), jnp.float32),
            dma(()), dma((slots,)), dma((slots,)), dma((2 * (pieces - 1),)), dma((2,)), dma((pieces,)), dma((2, 2)),
            dma((pieces,)), dma((pieces,)), dma((pieces,)), dma((slots,)), dma((slots,)),
            dma((2 * (pieces - 1),)), dma((2 * (pieces - 1),)), dma((2 * (pieces - 1),)), dma((2,)), dma((pieces,)),
        ],
        compiler_params=pltpu.CompilerParams(
            collective_id=step, has_side_effects=True, vmem_limit_bytes=60 * 1024 * 1024
        ),
        cost_estimate=pl.CostEstimate(
            flops=6 * (times + 1) * n_rows * n_cols * depth,
            bytes_accessed=4 * times * n_rows * n_cols,
            transcendentals=0,
        ),
    )(orbitals.reshape(pieces, chunk, depth), weight.T, screened)


def scatter_rows(value):
    n_col = lax.axis_size("col")
    if n_col & (n_col - 1):
        return lax.psum_scatter(value, "col", scatter_dimension=0, tiled=True)
    me = lax.axis_index("col")
    points = value.shape[0] // n_col
    value = value.reshape(n_col, points, value.shape[1])
    distance = 1
    while distance < n_col:
        bit = (me // distance) % 2
        pairs = value.reshape((value.shape[0] // 2, 2) + value.shape[1:])
        mine = lax.dynamic_index_in_dim(pairs, bit, 1, keepdims=False)
        theirs = lax.dynamic_index_in_dim(pairs, 1 - bit, 1, keepdims=False)
        swap = [(k, k ^ distance) for k in range(n_col)]
        value = mine + lax.ppermute(theirs, "col", swap)
        distance *= 2
    return value[0]


def body(orbitals, screened, green_weight, time_weight):
    n_row = lax.axis_size("row")
    n_col = lax.axis_size("col")
    factor = n_col // n_row
    points, depth = orbitals.shape
    weight = green_weight * time_weight[:, None]
    if n_row == 4 and n_col == 4 and points % 3 == 0 and (points // 3) % LANES == 0:
        for step in range(PASSES):
            orbitals = chain_pass(step, orbitals, weight, screened)
        return orbitals
    to_columns = [
        ((c // factor) * n_col + (c % factor) * n_row + m, m * n_col + c)
        for m in range(n_row)
        for c in range(n_col)
    ]
    ring = [(k, (k + 1) % n_row) for k in range(n_row)]
    me = lax.axis_index("row")
    parts = 1
    own = jnp.split(orbitals, parts, axis=1)
    for step in range(PASSES):
        piece = [lax.ppermute(o, ("row", "col"), to_columns) for o in own]
        rows = [lax.all_gather(o, "col", axis=0, tiled=True) for o in own]
        total = None
        if points % 128 == 0:
            for hop in range(n_row):
                later = None
                if hop < n_row - 1:
                    if total is not None:
                        piece, total = lax.optimization_barrier((piece, total))
                    later = [lax.ppermute(p, "row", ring) for p in piece]
                index = lax.rem(me - hop + n_row, n_row).astype(jnp.int32).reshape(1)
                total = apply_block(index, rows, piece, weight, screened, total)
                piece = later
        else:
            columns = [lax.all_gather(p, "row", axis=0, tiled=True) for p in piece]
            index = jnp.zeros((1,), jnp.int32)
            total = apply_block(index, rows, columns, weight, screened, None)
        own = [
            o - scatter_rows(v)
            for o, v in zip(own, total)
        ]
    return jnp.concatenate(own, axis=1)


def solution(mesh):
    in_specs = (P(("snap", "row", "col"), None), P("snap", "row", "col"), P("snap", None), P())
    out_specs = P(("snap", "row", "col"), None)
    return jax.shard_map(body, mesh=mesh, in_specs=in_specs, out_specs=out_specs, check_vma=False)
```

```python
import functools
import types

import jax
import jax.numpy as jnp
from jax import lax
from jax.experimental import pallas as pl
from jax.experimental.pallas import tpu as pltpu
from jax.sharding import PartitionSpec as P

PASSES = 2
LANES = 128


def split(value):
    high = value.astype(jnp.bfloat16)
    low = (value - high.astype(jnp.float32)).astype(jnp.bfloat16)
    return high, low


def apply_kernel(times, parts, has_total, index_ref, *refs):
    rows_refs, refs = refs[:parts], refs[parts:]
    cols_refs, refs = refs[:parts], refs[parts:]
    weight_ref, screened_ref, refs = refs[0], refs[1], refs[2:]
    total_refs = None
    if has_total:
        total_refs, refs = refs[:parts], refs[parts:]
    out_refs, (weighted, plain) = refs[:parts], refs[parts:]

    @pl.when(pl.program_id(0) == 0)
    def _():
        cols = jnp.concatenate([ref[...] for ref in cols_refs], axis=1)
        width, depth = cols.shape
        high, low = split(cols)
        plain[0:width, :] = high
        plain[width : 2 * width, :] = high
        plain[2 * width : 3 * width, :] = low
        for t in range(times):
            high, low = split((cols * weight_ref[t : t + 1, :]).T)
            weighted[t, 0:depth, :] = high
            weighted[t, depth : 2 * depth, :] = high
            weighted[t, 2 * depth : 3 * depth, :] = low

    high, low = split(jnp.concatenate([ref[...] for ref in rows_refs], axis=1))
    rows = jnp.concatenate([high, low, high], axis=1)
    mixed = None
    for t in range(times):
        green = jnp.dot(rows, weighted[t], preferred_element_type=jnp.float32)
        term = green * screened_ref[t]
        mixed = term if mixed is None else mixed + term
    high, low = split(mixed)
    mixed = jnp.concatenate([high, low, high], axis=1)
    applied = jnp.dot(mixed, plain[...], preferred_element_type=jnp.float32)
    part = applied.shape[1] // parts
    for k in range(parts):
        value = applied[:, k * part : (k + 1) * part]
        out_refs[k][...] = value + total_refs[k][...] if has_total else value


def apply_block(index, rows, cols, weight, screened, total):
    times = screened.shape[0]
    parts = len(rows)
    n_rows, part = rows[0].shape
    depth = parts * part
    width = cols[0].shape[0]
    tile = next(k for k in (512, 384, 256, 128, n_rows) if n_rows % k == 0)
    row_spec = pl.BlockSpec((tile, part), lambda i, ix: (i, 0))
    in_specs = [row_spec] * parts
    in_specs += [pl.BlockSpec((width, part), lambda i, ix: (0, 0))] * parts
    in_specs += [
        pl.BlockSpec((times, depth), lambda i, ix: (0, 0)),
        pl.BlockSpec((times, tile, width), lambda i, ix: (0, i, ix[0])),
    ]
    args = [index, *rows, *cols, weight, screened]
    if total is not None:
        in_specs += [row_spec] * parts
        args += total
    return pl.pallas_call(
        functools.partial(apply_kernel, times, parts, total is not None),
        out_shape=[jax.ShapeDtypeStruct((n_rows, part), jnp.float32)] * parts,
        grid_spec=pltpu.PrefetchScalarGridSpec(
            num_scalar_prefetch=1,
            grid=(n_rows // tile,),
            in_specs=in_specs,
            out_specs=[row_spec] * parts,
            scratch_shapes=[
                pltpu.VMEM((times, 3 * depth, width), jnp.bfloat16),
                pltpu.VMEM((3 * width, depth), jnp.bfloat16),
            ],
        ),
        compiler_params=pltpu.CompilerParams(
            dimension_semantics=("arbitrary",), vmem_limit_bytes=56 * 1024 * 1024
        ),
        cost_estimate=pl.CostEstimate(
            flops=6 * (times + 1) * n_rows * width * depth,
            bytes_accessed=4 * (times * n_rows * width + 3 * n_rows * depth),
            transcendentals=0,
        ),
    )(*args)


def chain_kernel(
    passes, times, own_ref, weight_ref, screened_ref, out_ref,
    buf, rows, weighted, plain, acc, from_partner, from_twin, tiles, turned_weight,
    own_sem, row_recv, col_recv, side_recv, partner_recv, twin_recv, tile_sem,
    partner_send, twin_send, relay_send, down_send, up_send,
    side_down_send, side_up_send, cross_send, sum_send, twin_sum_send,
):
    n = lax.axis_size("row")
    r = lax.axis_index("row")
    c = lax.axis_index("col")
    x, k = c // 2, c % 2
    partner, twin, opposite = c + 1 - 2 * k, c + 2 - 4 * x, 3 - c
    pieces, chunk, depth = own_ref.shape
    slots = n * pieces
    points = pieces * chunk
    units = slots // 2
    half_units = units // 2
    diagonal = r == c
    base = jnp.where(diagonal, 0, slots)
    goes_down = (r >= c) & (r < n - 1)
    goes_up = (r <= c) & (r > 0)
    relays = (goes_down | goes_up) & jnp.logical_not(diagonal)
    distance = jnp.where(r > c, r - c, c - r)
    near = relays & (distance == 1)
    far = relays & jnp.logical_not(near)

    stride = 2 * slots + 2 * (pieces - 1)
    side_count = pieces - 1
    steps = units * n
    whole = half_units * n

    def remote(source, target, send, recv, row, col):
        return pltpu.make_async_remote_copy(
            src_ref=source, dst_ref=target, send_sem=send, recv_sem=recv,
            device_id={"row": row, "col": col}, device_id_type=pl.DeviceIdType.MESH,
        )

    def side_set(e):
        return 2 * (1 - x) + e

    def side_goes_down(e):
        return (r >= side_set(e)) & (r < n - 1)

    def side_goes_up(e):
        return (r <= side_set(e)) & (r > 0)

    def unit_slots(u):
        half = jnp.where((u == 2) | (u >= 4), 1, 0)
        piece = ((u + 1) // 2) % pieces
        block = 2 * ((x + half) % 2)
        return block * pieces + piece, (block + 1) * pieces + piece

    def place_of(step):
        late = step - whole
        second = jnp.where(late < units, late, late - units)
        u = jnp.where(step < whole, step // n, half_units + second // 2)
        m = jnp.where(step < whole, step % n, second % 2 + jnp.where(late < units, 0, 2))
        return u, m

    def tile_of(m):
        return 2 * ((x + 1 + m // 2) % 2) + (k + 1 + m) % 2

    def tile_copies(step):
        u, m = place_of(step)
        slot = step % 2
        first = pl.multiple_of(tile_of(m) * points, chunk)
        return [
            pltpu.make_async_copy(
                screened_ref.at[:, pl.ds(first, points), pl.ds(pl.multiple_of(q * chunk, chunk), chunk)],
                tiles.at[slot, :, :, pl.ds(j * chunk, chunk)],
                tile_sem.at[slot, j],
            )
            for j, q in enumerate(unit_slots(u))
        ]

    def moves(p):
        at = p * stride

        def to_partner(i):
            q = c * pieces + i
            return remote(buf.at[at + q], buf.at[at + q], partner_send.at[i], row_recv.at[p * slots + q], r, partner)

        def to_twin(i):
            q = c * pieces + i
            return remote(buf.at[at + q], buf.at[at + q], twin_send.at[i], row_recv.at[p * slots + q], r, twin)

        def relay(i):
            q = twin * pieces + i
            return remote(buf.at[at + q], buf.at[at + q], relay_send.at[i], row_recv.at[p * slots + q], r, partner)

        def wait_row(col, i):
            q = col * pieces + i
            remote(buf.at[at + q], buf.at[at + q], partner_send.at[i], row_recv.at[p * slots + q], r, partner).wait_recv()

        def down(q):
            return remote(buf.at[at + base + q], buf.at[at + slots + q], down_send.at[q], col_recv.at[p * slots + q], r + 1, c)

        def up(q):
            return remote(buf.at[at + base + q], buf.at[at + slots + q], up_send.at[q], col_recv.at[p * slots + q], r - 1, c)

        def wait_col(q):
            remote(buf.at[at + slots + q], buf.at[at + slots + q], down_send.at[q], col_recv.at[p * slots + q], r, partner).wait_recv()

        def forward(q):
            @pl.when(goes_down)
            def _():
                down(q).start()

            @pl.when(goes_up)
            def _():
                up(q).start()

        def side_source(e, i):
            own = c * pieces + i
            place = 2 * slots + e * side_count + i - 1
            return buf.at[at + jnp.where(r == side_set(e), own, place)]

        def side_down(e, i):
            j = e * side_count + i - 1
            return remote(side_source(e, i), buf.at[at + 2 * slots + j], side_down_send.at[j], side_recv.at[p * 2 * side_count + j], r + 1, c)

        def side_up(e, i):
            j = e * side_count + i - 1
            return remote(side_source(e, i), buf.at[at + 2 * slots + j], side_up_send.at[j], side_recv.at[p * 2 * side_count + j], r - 1, c)

        def side_cross(e, i):
            j = e * side_count + i - 1
            q = c * pieces + i
            return remote(buf.at[at + 2 * slots + j], buf.at[at + slots + q], cross_send.at[j], col_recv.at[p * slots + q], r, side_set(e))

        def side_forward(e, i):
            @pl.when(side_goes_down(e))
            def _():
                side_down(e, i).start()

            @pl.when(side_goes_up(e))
            def _():
                side_up(e, i).start()

        def side_serve(i):
            for e in range(2):
                @pl.when(r != side_set(e))
                def _():
                    j = e * side_count + i - 1
                    here = buf.at[at + 2 * slots + j]
                    remote(here, here, cross_send.at[j], side_recv.at[p * 2 * side_count + j], r, partner).wait_recv()
                    side_forward(e, i)
                    side_cross(e, i).start()

        def serve(u):
            for q in unit_slots(u):
                wait_col(q)
                forward(q)

        def split_rows(col):
            @pl.loop(0, pieces)
            def _(i):
                q = col * pieces + i
                first = pl.multiple_of(q * chunk, chunk)
                high, low = split(buf[at + q])
                rows[pl.ds(first, chunk), 0:depth] = high
                rows[pl.ds(first, chunk), depth : 2 * depth] = low

        def partner_sum(j):
            block = opposite if j == 0 else partner
            return remote(acc.at[block], from_partner.at[2 * p + j], sum_send.at[j], partner_recv.at[2 * p + j], r, partner)

        def twin_sum(i):
            part = pl.ds(i * chunk, chunk)
            return remote(acc.at[twin, part], from_twin.at[p, part], twin_sum_send.at[i], twin_recv.at[p * pieces + i], r, twin)

        def launch(i):
            to_twin(i).start()
            to_partner(i).start()

            @pl.when(diagonal)
            def _():
                forward(c * pieces + i)

            if i > 0:
                for e in range(2):
                    @pl.when(r == side_set(e))
                    def _():
                        side_forward(e, i)

        return types.SimpleNamespace(**locals())

    own_copy = pltpu.make_async_copy(own_ref, buf.at[pl.ds(c * pieces, pieces)], own_sem)
    own_copy.start()
    barrier = pltpu.get_barrier_semaphore()
    for col in (partner, twin, opposite):
        pl.semaphore_signal(
            barrier, inc=1, device_id={"row": r, "col": col}, device_id_type=pl.DeviceIdType.MESH
        )

    @pl.when(r > 0)
    def _():
        pl.semaphore_signal(
            barrier, inc=1, device_id={"row": r - 1, "col": c}, device_id_type=pl.DeviceIdType.MESH
        )

    @pl.when(r < n - 1)
    def _():
        pl.semaphore_signal(
            barrier, inc=1, device_id={"row": r + 1, "col": c}, device_id_type=pl.DeviceIdType.MESH
        )

    own_copy.wait()
    pl.semaphore_wait(barrier, 3 + jnp.where(r > 0, 1, 0) + jnp.where(r < n - 1, 1, 0))

    turned_weight[...] = weight_ref[...].T
    acc[...] = jnp.zeros_like(acc)
    first_pass = moves(0)
    for i in range(pieces):
        first_pass.launch(i)

    @pl.loop(0, passes)
    def _(p):
        v = moves(p)
        for copy in tile_copies(0):
            copy.start()

        for i in range(pieces):
            v.wait_row(partner, i)

            @pl.when(diagonal)
            def _():
                v.forward(partner * pieces + i)

        v.split_rows(c)
        v.split_rows(partner)
        for i in range(pieces):
            for col in (twin, opposite):
                v.wait_row(col, i)
                if col is twin:
                    v.relay(i).start()
                if i == 0:
                    @pl.when(diagonal)
                    def _():
                        v.forward(col * pieces + i)

            if i > 0:
                @pl.when(near)
                def _():
                    v.serve(i - 1)

        v.side_serve(1)
        v.split_rows(twin)
        v.split_rows(opposite)

        @pl.when(far)
        def _():
            v.serve(0)

        @pl.loop(0, steps)
        def _(step):
            u, m = place_of(step)
            keep = jnp.where(u < half_units, 0, u - half_units)

            for unit, near_step, far_step in ((1, steps, 4), (3, 5, 9), (5, 10, 15)):
                @pl.when(relays & (step == jnp.where(near, near_step, far_step)))
                def _():
                    v.serve(unit)

            @pl.when(step == n)
            def _():
                v.side_serve(2)

            @pl.when(step + 1 < steps)
            def _():
                for copy in tile_copies(step + 1):
                    copy.start()

            @pl.when((m == 0) & (step < whole + units))
            def _():
                first, second = unit_slots(u)

                @pl.when(jnp.logical_not(diagonal) & (jnp.logical_not(relays) | (u == 2) | (u == 4)))
                def _():
                    v.wait_col(first)
                    v.wait_col(second)

                cols = jnp.concatenate([buf[v.at + base + first], buf[v.at + base + second]], axis=0)
                width = cols.shape[0]
                high, low = split(cols)
                plain[keep, 0:width, :] = high
                plain[keep, width : 2 * width, :] = high
                plain[keep, 2 * width : 3 * width, :] = low
                turned = cols.T
                for t in range(times):
                    high, low = split(turned * turned_weight[:, t : t + 1])
                    weighted[keep, t, 0:depth, :] = high
                    weighted[keep, t, depth : 2 * depth, :] = high
                    weighted[keep, t, 2 * depth : 3 * depth, :] = low

            for copy in tile_copies(step):
                copy.wait()
            tile = tile_of(m)
            left = rows[pl.ds(pl.multiple_of(tile * points, chunk), points), :]
            left = jnp.concatenate([left, left[:, 0:depth]], axis=1)
            mixed = None
            for t in range(times):
                green = jnp.dot(left, weighted[keep, t], preferred_element_type=jnp.float32)
                term = green * tiles[step % 2, t]
                mixed = term if mixed is None else mixed + term
            high, low = split(mixed)
            mixed = jnp.concatenate([high, low, high], axis=1)
            acc[tile] = jnp.where(u == 0, 0.0, acc[tile]) + jnp.dot(mixed, plain[keep], preferred_element_type=jnp.float32)

            @pl.when((u == units - 1) & (m == 0))
            def _():
                v.partner_sum(0).start()

            @pl.when((u == units - 1) & (m == 1))
            def _():
                v.partner_sum(0).wait_recv()
                for i in range(pieces):
                    part = slice(i * chunk, (i + 1) * chunk)
                    acc[twin, part, :] = acc[twin, part, :] + from_partner[2 * p, part, :]
                    v.twin_sum(i).start()

            @pl.when((u == units - 1) & (m == 2))
            def _():
                v.partner_sum(1).start()

        for i in range(pieces):
            v.to_twin(i).wait_send()
            v.to_partner(i).wait_send()
            v.relay(i).wait_send()

        for i in range(1, pieces):
            for e in range(2):
                @pl.when(side_goes_down(e))
                def _():
                    v.side_down(e, i).wait_send()

                @pl.when(side_goes_up(e))
                def _():
                    v.side_up(e, i).wait_send()

                @pl.when(r != side_set(e))
                def _():
                    v.side_cross(e, i).wait_send()

        for u in (0, 1, 3, 5):
            for q in unit_slots(u):
                @pl.when(goes_down)
                def _():
                    v.down(q).wait_send()

                @pl.when(goes_up)
                def _():
                    v.up(q).wait_send()

        v.partner_sum(1).wait_recv()
        for i in range(pieces):
            part = slice(i * chunk, (i + 1) * chunk)
            mine = acc[c, part, :] + from_partner[2 * p + 1, part, :]
            v.twin_sum(i).wait_recv()
            updated = buf[v.at + c * pieces + i] - (mine + from_twin[p, part, :])

            @pl.when(p == passes - 1)
            def _():
                out_ref[part, :] = updated

            @pl.when(p < passes - 1)
            def _():
                later = moves(p + 1)
                buf[later.at + c * pieces + i] = updated
                later.launch(i)

        for i in range(pieces):
            v.twin_sum(i).wait_send()
        for j in range(2):
            v.partner_sum(j).wait_send()


def chain_passes(orbitals, weight, screened):
    times, n_rows, n_cols = screened.shape
    points, depth = orbitals.shape
    n = n_rows // points
    pieces = 3
    chunk = points // pieces
    slots = n * pieces
    sides = 2 * (pieces - 1)
    weight = jnp.pad(weight, ((0, -times % 8), (0, 0)))
    dma = pltpu.SemaphoreType.DMA
    return pl.pallas_call(
        functools.partial(chain_kernel, PASSES, times),
        out_shape=jax.ShapeDtypeStruct((points, depth), jnp.float32),
        in_specs=[
            pl.BlockSpec(memory_space=pl.ANY),
            pl.BlockSpec(memory_space=pltpu.VMEM),
            pl.BlockSpec(memory_space=pl.ANY),
        ],
        out_specs=pl.BlockSpec(memory_space=pltpu.VMEM),
        scratch_shapes=[
            pltpu.VMEM((PASSES * (2 * slots + sides), chunk, depth), jnp.float32),
            pltpu.VMEM((n_rows, 2 * depth), jnp.bfloat16),
            pltpu.VMEM((pieces, times, 3 * depth, 2 * chunk), jnp.bfloat16),
            pltpu.VMEM((pieces, 6 * chunk, depth), jnp.bfloat16),
            pltpu.VMEM((n, points, depth), jnp.float32),
            pltpu.VMEM((PASSES * 2, points, depth), jnp.float32),
            pltpu.VMEM((PASSES, points, depth), jnp.float32),
            pltpu.VMEM((2, times, points, 2 * chunk), jnp.float32),
            pltpu.VMEM((depth, weight.shape[0]), jnp.float32),
            dma(()), dma((PASSES * slots,)), dma((PASSES * slots,)), dma((PASSES * sides,)),
            dma((PASSES * 2,)), dma((PASSES * pieces,)), dma((2, 2)),
            dma((pieces,)), dma((pieces,)), dma((pieces,)), dma((slots,)), dma((slots,)),
            dma((sides,)), dma((sides,)), dma((sides,)), dma((2,)), dma((pieces,)),
        ],
        compiler_params=pltpu.CompilerParams(
            collective_id=0, has_side_effects=True, vmem_limit_bytes=60 * 1024 * 1024
        ),
        cost_estimate=pl.CostEstimate(
            flops=PASSES * 6 * (times + 1) * n_rows * n_cols * depth,
            bytes_accessed=PASSES * 4 * times * n_rows * n_cols,
            transcendentals=0,
        ),
    )(orbitals.reshape(pieces, chunk, depth), weight, screened)


def scatter_rows(value):
    n_col = lax.axis_size("col")
    if n_col & (n_col - 1):
        return lax.psum_scatter(value, "col", scatter_dimension=0, tiled=True)
    me = lax.axis_index("col")
    points = value.shape[0] // n_col
    value = value.reshape(n_col, points, value.shape[1])
    distance = 1
    while distance < n_col:
        bit = (me // distance) % 2
        pairs = value.reshape((value.shape[0] // 2, 2) + value.shape[1:])
        mine = lax.dynamic_index_in_dim(pairs, bit, 1, keepdims=False)
        theirs = lax.dynamic_index_in_dim(pairs, 1 - bit, 1, keepdims=False)
        swap = [(k, k ^ distance) for k in range(n_col)]
        value = mine + lax.ppermute(theirs, "col", swap)
        distance *= 2
    return value[0]


def body(orbitals, screened, green_weight, time_weight):
    n_row = lax.axis_size("row")
    n_col = lax.axis_size("col")
    factor = n_col // n_row
    points, depth = orbitals.shape
    weight = green_weight * time_weight[:, None]
    if n_row == 4 and n_col == 4 and points % 3 == 0 and (points // 3) % LANES == 0:
        return chain_passes(orbitals, weight, screened)
    to_columns = [
        ((c // factor) * n_col + (c % factor) * n_row + m, m * n_col + c)
        for m in range(n_row)
        for c in range(n_col)
    ]
    ring = [(k, (k + 1) % n_row) for k in range(n_row)]
    me = lax.axis_index("row")
    parts = 1
    own = jnp.split(orbitals, parts, axis=1)
    for step in range(PASSES):
        piece = [lax.ppermute(o, ("row", "col"), to_columns) for o in own]
        rows = [lax.all_gather(o, "col", axis=0, tiled=True) for o in own]
        total = None
        if points % 128 == 0:
            for hop in range(n_row):
                later = None
                if hop < n_row - 1:
                    if total is not None:
                        piece, total = lax.optimization_barrier((piece, total))
                    later = [lax.ppermute(p, "row", ring) for p in piece]
                index = lax.rem(me - hop + n_row, n_row).astype(jnp.int32).reshape(1)
                total = apply_block(index, rows, piece, weight, screened, total)
                piece = later
        else:
            columns = [lax.all_gather(p, "row", axis=0, tiled=True) for p in piece]
            index = jnp.zeros((1,), jnp.int32)
            total = apply_block(index, rows, columns, weight, screened, None)
        own = [
            o - scatter_rows(v)
            for o, v in zip(own, total)
        ]
    return jnp.concatenate(own, axis=1)


def solution(mesh):
    in_specs = (P(("snap", "row", "col"), None), P("snap", "row", "col"), P("snap", None), P())
    out_specs = P(("snap", "row", "col"), None)
    return jax.shard_map(body, mesh=mesh, in_specs=in_specs, out_specs=out_specs, check_vma=False)
```
